32 devices in a mesh: groups: 2 (over x), ctx: 16 (over z, y, core).
Axes of the slice: x: 2, y: 2, z: 4, core: 2. Of those that a mesh axis runs over, the one named last changes fastest.
Arguments:
- queries: bfloat16 [8192, 2560], P(('groups', 'ctx')), parts along dimension 0, may hold values from -6 to 6
- keys: bfloat16 [8192, 2560], P(('groups', 'ctx')), parts along dimension 0, may hold values from -6 to 6
- values: bfloat16 [8192, 2560], P(('groups', 'ctx')), parts along dimension 0, may hold values from -6 to 6
- kv_lists: int32 [16, 4, 2, 8], P('ctx'), may hold values from 0 to 7, as said below
- kv_counts: int32 [16, 4, 2], P('ctx'), may hold values from 0 to 8, as said below
Outputs:
- attended: bfloat16 [8192, 2560], P(('groups', 'ctx')), parts along dimension 0
The draws below stay inside these ranges and needn't reach their ends.
There are 2 independent parts, one for each index of `groups`. The reference program is written for one: setup_inputs(seed, part) draws one part's arguments, and reference() takes and returns one part's arrays. A program takes and returns all parts, laid end to end along the dimension named above; an argument that names none is the same for every part. Nothing has to cross between parts.
Inputs may be any that keep to these rules, and one draw needn't show every extreme that they name: For every device d, level k and side s, the first 8 // 2**k entries of kv_lists[d, k, s] are distinct block indices; later entries are never read. kv_counts[d, k, s] is at most 8 // 2**k and reaches it for some device at every level and side; it is 0 exactly where the partner d - 2**k (s = 0) or d + 2**k (s = 1) lies outside 0 to 15, else 1 or more.
All inputs are finite; a program needn't handle non-finite values.
Results may differ from the reference program's by a relative error of at most 0.005.
Values may be sent and summed in bfloat16 or wider, within the bound.
A program may use at most 128 MiB of HBM per device.

```python
import math
import jax
import jax.numpy as jnp
from jax import lax

HEADS = 20
HEAD = 128
ROWS = 256
NBLK = 8
LEVELS = 4
BS = 32
TOKENS = 4096
N_CTX = 16


def draw_queries(key, part):
    base_rows = jax.random.normal(jax.random.fold_in(key, 1), (TOKENS, HEADS * HEAD), jnp.float32) * 1.8
    return jnp.clip(base_rows, -6.0, 6.0).astype(jnp.bfloat16)


def draw_keys(key, part):
    base_rows = jax.random.normal(jax.random.fold_in(key, 2), (TOKENS, HEADS * HEAD), jnp.float32)
    return jnp.clip(base_rows, -6.0, 6.0).astype(jnp.bfloat16)


def draw_kv_lists(key, part):
    random_keys = jax.random.randint(jax.random.fold_in(key, 21), (N_CTX, LEVELS, 2, NBLK), 0, 1 << 20)
    random_keys = random_keys * NBLK + jnp.arange(NBLK, dtype=jnp.int32)
    return jnp.argsort(random_keys, axis=-1).astype(jnp.int32)


def draw_kv_counts(key, part):
    device_ids = jnp.arange(N_CTX, dtype=jnp.int32)[:, None, None]
    level_ids = jnp.arange(LEVELS, dtype=jnp.int32)[None, :, None]
    side_ids = jnp.arange(2, dtype=jnp.int32)[None, None, :]
    distance = jnp.left_shift(jnp.int32(1), level_ids)
    partner = jnp.where(side_ids == 0, device_ids - distance, device_ids + distance)
    present = (partner >= 0) & (partner < N_CTX)
    capacity = NBLK // distance
    random_pick = jax.random.randint(jax.random.fold_in(key, 22), (N_CTX, LEVELS, 2), 0, 1 << 20) % capacity + 1
    saturated = device_ids % 4 == 0
    counted = jnp.where(present, jnp.where(saturated, capacity, random_pick), 0)
    return counted.astype(jnp.int32)


def shard_levels(rng, shape, shards, low, top_value):
    def one(position, parts):
        steps = jax.random.uniform(jax.random.fold_in(jax.random.fold_in(rng, 6), position), (parts,), jnp.float32, low / len(shards), top_value / len(shards))
        return jnp.repeat(jnp.exp(steps), shape[position] // parts).reshape((-1,) + (1,) * (len(shape) - position - 1))

    level = one(*shards[0])
    for cut in shards[1:]:
        level = level * one(*cut)
    return level


def noise(own_key, extent, deviation, limit, split=(), kind=jnp.bfloat16):
    values = deviation * jax.random.normal(own_key, extent, jnp.float32)
    if split:
        values = values * shard_levels(own_key, extent, split, -0.22, 0.18)
    return jnp.clip(values, -limit, limit).astype(kind)


def setup_inputs(seed: int = 0, part: int = 0) -> dict:
    streams_of = jax.random.split(jax.random.key(seed), 6)
    part_splits = jax.random.split(jax.random.fold_in(streams_of[5], part), 6)
    return {
        "queries": draw_queries(jax.random.fold_in(jax.random.fold_in(streams_of[5], part), 71), part),
        "keys": draw_keys(jax.random.fold_in(jax.random.fold_in(streams_of[5], part), 71), part),
        "values": noise(part_splits[2], (TOKENS, HEADS * HEAD), 1.0, 6.0, ((0, 16),)),
        "kv_lists": draw_kv_lists(jax.random.fold_in(streams_of[5], 71), part),
        "kv_counts": draw_kv_counts(jax.random.fold_in(streams_of[5], 71), part),
    }


def reference(queries, keys, values, kv_lists, kv_counts):
    width = HEADS * HEAD
    key_blocks = keys.reshape(N_CTX, NBLK, BS, width)
    value_blocks = values.reshape(N_CTX, NBLK, BS, width)

    def one_device(device_id):
        query_rows = lax.dynamic_slice_in_dim(queries, device_id * ROWS, ROWS, 0)
        key_parts = [key_blocks[device_id].reshape(ROWS, width)]
        value_parts = [value_blocks[device_id].reshape(ROWS, width)]
        flag_parts = [jnp.ones((ROWS,), dtype=bool)]
        for level_id in range(LEVELS):
            distance = 2 ** level_id
            capacity = NBLK // distance
            for side_id in range(2):
                partner = device_id - distance if side_id == 0 else device_id + distance
                safe_partner = jnp.clip(partner, 0, N_CTX - 1).astype(jnp.int32)
                chosen = kv_lists[device_id, level_id, side_id, :capacity].astype(jnp.int32)
                counted = kv_counts[device_id, level_id, side_id]
                key_parts.append(key_blocks[safe_partner][chosen].reshape(capacity * BS, width))
                value_parts.append(value_blocks[safe_partner][chosen].reshape(capacity * BS, width))
                slot_ids = jnp.arange(capacity * BS, dtype=jnp.int32) // BS
                flag_parts.append(slot_ids < counted)
        all_keys = jnp.concatenate(key_parts, axis=0).astype(jnp.float32)
        all_values = jnp.concatenate(value_parts, axis=0).astype(jnp.float32)
        allowed = jnp.concatenate(flag_parts, axis=0)
        query_heads = query_rows.astype(jnp.float32).reshape(ROWS, HEADS, HEAD)
        key_heads = all_keys.reshape(-1, HEADS, HEAD)
        value_heads = all_values.reshape(-1, HEADS, HEAD)
        scores = jnp.einsum('qhd,khd->hqk', query_heads, key_heads) * (1.0 / math.sqrt(HEAD))
        scores = jnp.where(allowed[None, None, :], scores, -1e+30)
        top_score = lax.optimization_barrier(jnp.max(scores, axis=-1, keepdims=True))
        weights = jnp.exp(scores - top_score)
        weight_total = lax.optimization_barrier(jnp.sum(weights, axis=-1))
        rounded = lax.optimization_barrier(weights.astype(jnp.bfloat16)).astype(jnp.float32)
        mixed_values = jnp.einsum('hqk,khd->qhd', rounded, value_heads)
        result = mixed_values / jnp.transpose(weight_total)[:, :, None]
        return result.reshape(ROWS, width).astype(jnp.bfloat16)
    results = lax.map(one_device, jnp.arange(N_CTX, dtype=jnp.int32))
    return results.reshape(TOKENS, width)
```

```python
import functools
import math

import jax
import jax.numpy as jnp
from jax import lax
from jax.experimental import pallas as pl
from jax.experimental.pallas import tpu as pltpu
from jax.sharding import PartitionSpec as P

HEAD = 128
MASKED = -1e30
PIECE_HEADS = 2
MESH = pl.DeviceIdType.MESH


def body(
    n_ctx, nblk, piece,
    q_hbm, k_hbm, v_hbm, lists, counts, out_ref,
    q_ref, k_ref, v_ref,
    near, across, passed, skew, skew_pack, far, far_pack, stage,
    q_got, o_send, o_got, lse_send, lse_got,
    acc, top, tot, bias_near, bias_late, bias_guest, lists_got, counts_got,
    s_list, s_count, s_near, s_across, s_passed, s_skew, s_far, s_q, s_o, s_lse,
    r_own, r_list, r_count, r_near, r_across, r_passed, r_skew, r_far, r_q, r_o, r_lse,
):
    own = [
        pltpu.make_async_copy(src, dst, r_own.at[i])
        for i, (src, dst) in enumerate(((k_hbm, k_ref), (v_hbm, v_ref), (q_hbm, q_ref)))
    ]
    for copy in own:
        copy.start()
    rows, width = q_ref.shape
    heads = width // HEAD
    bs = rows // nblk
    cap1, cap2, cap3 = nblk // 2, nblk // 4, nblk // 8
    rate = math.log2(math.e) / math.sqrt(HEAD)
    cols_piece = piece * HEAD
    pieces = heads // piece
    far_room = far.shape[1] * bs

    d = lax.axis_index("ctx")
    place = lax.rem(d, 4)
    quad = d // 4
    quads = n_ctx // 4
    left = place < 2
    s = jnp.where(left, 1, -1)
    gate = (place == 1) | (place == 2)
    outer = jnp.logical_not(gate)
    has_out = jnp.where(left, quad > 0, quad < quads - 1)
    has_in = jnp.where(left, quad < quads - 1, quad > 0)
    side_in = jnp.where(left, 1, 0)
    side_out = 1 - side_in
    twin = jnp.where(gate, d - s, d + s)
    across_to = jnp.where(gate, d + s, d + 3 * s)
    hosts = outer & has_in
    guests = outer & has_out
    gets_skew = gate & has_out

    fars = []
    for distance in (4, 8):
        fars.append((d + distance, d + distance < n_ctx))
        fars.append((d - distance, d - distance >= 0))
    arrives = [fars[1], fars[0], fars[3], fars[2]]
    far_rows = (cap2 * bs, cap2 * bs, cap3 * bs, cap3 * bs)
    far_start = (0, cap2 * bs, 2 * cap2 * bs, (2 * cap2 + cap3) * bs)
    far_blocks = [pl.ds(a // bs, n // bs) for a, n in zip(far_start, far_rows)]
    hosted = (outer & left, outer & jnp.logical_not(left), jnp.bool_(False), jnp.bool_(False))
    far_sends = [ok & jnp.logical_not(hosted[i]) for i, (_, ok) in enumerate(fars)]
    far_gets = [ok & jnp.logical_not(hosted[i]) for i, (_, ok) in enumerate(arrives)]
    guest_slot = jnp.where(left, 0, 1)

    def to(device):
        return {"ctx": device}

    barrier = pltpu.get_barrier_semaphore()
    always = jnp.bool_(True)
    partners = [(p, ok) for p, ok in fars]
    partners += [
        (twin, always),
        (across_to, always),
        (d + 5 * s, hosts),
        (d - 5 * s, gets_skew),
    ]
    count = jnp.int32(0)
    for p, ok in partners:
        count = count + ok.astype(jnp.int32)

        @pl.when(ok)
        def _(p=p):
            pl.semaphore_signal(barrier, inc=1, device_id=to(p), device_id_type=MESH)

    pl.semaphore_wait(barrier, count)

    def remote(src, dst, ssem, rsem, device):
        return pltpu.make_async_remote_copy(
            src_ref=src, dst_ref=dst, send_sem=ssem, recv_sem=rsem,
            device_id=to(device), device_id_type=MESH,
        )

    def span(c):
        return pl.ds(pl.multiple_of(c * cols_piece, cols_piece), cols_piece)

    flip = (1, 0, 3, 2)

    def list_copy(slot, device):
        return remote(lists.at[0], lists_got.at[slot], s_list.at[slot], r_list.at[slot], device)

    def count_copy():
        return remote(counts, counts_got, s_count, r_count, d - 4 * s)

    def near_copy(kv):
        return remote((k_hbm, v_hbm)[kv], near.at[kv], s_near.at[kv], r_near.at[kv], twin)

    def across_copy(c, kv):
        x = span(c)
        return remote(
            (k_hbm, v_hbm)[kv].at[:, :, x], across.at[kv, :, :, x], s_across, r_across.at[kv, c], across_to
        )

    def passed_copy(c):
        x = span(c)
        return remote(across.at[:, :, :, x], passed.at[:, :, :, x], s_passed, r_passed.at[c], twin)

    def skew_copy(c):
        x = span(c)
        return remote(skew_pack.at[:, :, :, x], skew.at[:, :, :, x], s_skew, r_skew.at[c], d + 5 * s)

    def far_copy(i, c):
        r, x = far_blocks[i], span(c)
        return remote(
            far_pack.at[:, r, :, x], far.at[:, r, :, x], s_far.at[i], r_far.at[i, c], fars[i][0]
        )

    def q_copy(c):
        x = span(c)
        return remote(q_hbm.at[:, x], q_got.at[:, x], s_q, r_q.at[c], d - 4 * s)

    def o_copy(c):
        x = span(c)
        return remote(o_send.at[:, x], o_got.at[:, x], s_o, r_o.at[c], d + 4 * s)

    def lse_copy(c):
        h = pl.ds(c * piece, piece)
        return remote(lse_send.at[h], lse_got.at[h], s_lse, r_lse.at[c], d + 4 * s)

    def each_piece(one):
        def step(c, carry):
            one(c)
            return carry

        lax.fori_loop(0, pieces, step, 0)

    list_sends = [(flip[i], p, ok) for i, (p, ok) in enumerate(fars)] + [(4, d - 5 * s, gets_skew)]
    list_gets = [(i, p, ok) for i, (p, ok) in enumerate(fars)] + [(4, d + 5 * s, hosts)]
    for slot, p, ok in list_sends:
        @pl.when(ok)
        def _(slot=slot, p=p):
            list_copy(slot, p).start()

    @pl.when(guests)
    def _():
        count_copy().start()

    def start_across(c):
        for kv in range(2):
            across_copy(c, kv).start()

    each_piece(start_across)
    for kv in range(2):
        near_copy(kv).start()

    for i in range(4):
        @pl.when(jnp.logical_not(far_gets[i]))
        def _(i=i):
            for kv in range(2):
                far[kv, far_blocks[i]] = jnp.zeros((far_rows[i] // bs, bs, width), far.dtype)

    spare = far_room - sum(far_rows)
    if spare:
        for kv in range(2):
            far[kv, pl.ds(sum(far_rows) // bs, spare // bs)] = jnp.zeros(
                (spare // bs, bs, width), far.dtype
            )

    @pl.when(gate & jnp.logical_not(has_out))
    def _():
        for kv in range(2):
            skew[kv] = jnp.zeros(skew.shape[1:], skew.dtype)

    @pl.when(outer & jnp.logical_not(has_out))
    def _():
        o_got[...] = jnp.zeros(o_got.shape, o_got.dtype)
        lse_got[...] = jnp.full(lse_got.shape, MASKED, lse_got.dtype)

    for copy in own:
        copy.wait()

    def flat(x):
        return x.reshape(x.shape[0] * x.shape[1], x.shape[2])

    for i, p, ok in list_gets:
        @pl.when(ok)
        def _(i=i, p=p):
            list_copy(i, p).wait_recv()
            if i < 4:
                for j in range(far_rows[i] // bs):
                    source = lists_got[i, 2 + i // 2, i % 2, j]
                    far_pack[0, far_start[i] // bs + j] = k_ref[source]
                    far_pack[1, far_start[i] // bs + j] = v_ref[source]

    @pl.when(hosts)
    def _():
        count_copy().wait_recv()

    def start_far(c):
        @pl.when(guests)
        def _():
            q_copy(c).start()

        for i in range(4):
            @pl.when(far_sends[i])
            def _(i=i):
                far_copy(i, c).start()

    each_piece(start_far)

    def as_bias(seen):
        return jnp.where(seen, 0.0, MASKED).astype(jnp.float32)

    def full_bias(listed, counted):
        block = lax.broadcasted_iota(jnp.int32, (1, rows), 1) // bs
        seen = jnp.zeros((1, rows), jnp.int32)
        for j in range(nblk):
            hit = (block == listed(j)) & (jnp.full((1, rows), j) < counted)
            seen = seen + hit.astype(jnp.int32)
        return as_bias(seen > 0)

    def listed_bias(n, counted):
        column = lax.broadcasted_iota(jnp.int32, (1, n), 1)
        return as_bias(column < counted * bs)

    half = cap1 * bs
    quarter = cap2 * bs
    side_near = jnp.where(gate, side_out, side_in)
    bias_near[...] = full_bias(lambda j: lists[0, 0, side_near, j], counts[0, side_near, 0])
    column = lax.broadcasted_iota(jnp.int32, (1, far_room), 1)
    limit = jnp.zeros(column.shape, jnp.int32)
    for i in range(4):
        shown = jnp.where(far_gets[i], counts[0, i % 2, 2 + i // 2], 0)
        limit = jnp.where(column >= far_start[i], far_start[i] + shown * bs, limit)
    limit = jnp.where(column >= sum(far_rows), 0, limit)
    bias_late[:, :far_room] = as_bias(column < limit)
    bias_late[:, far_room:far_room + half] = listed_bias(half, counts[0, side_in, 1])
    bias_late[:, far_room + half:far_room + 2 * half] = listed_bias(half, counts[0, side_out, 1])
    bias_late[:, far_room + 2 * half:] = full_bias(
        lambda j: lists[0, 0, side_in, j], counts[0, side_in, 0]
    )

    @pl.when(hosts)
    def _():
        bias_guest[:, :rows] = full_bias(
            lambda j: lists_got[guest_slot, 0, side_out, j], counts_got[0, side_out, 0]
        )
        bias_guest[:, rows:rows + half] = listed_bias(half, counts_got[0, side_out, 1])
        bias_guest[:, rows + half:] = listed_bias(
            bias_guest.shape[1] - rows - half, counts_got[0, side_out, 2]
        )

    def wide(x, n):
        return jnp.concatenate([x] * (n // HEAD), axis=1)

    def folded(p):
        total = p[:, :HEAD]
        for i in range(1, p.shape[1] // HEAD):
            total = total + p[:, i * HEAD:(i + 1) * HEAD]
        return total

    def scores(q, k):
        return lax.dot_general(
            q, k, (((1,), (1,)), ((), ())), preferred_element_type=jnp.float32
        ) * rate

    def weigh(sc, v, old=None):
        n = sc.shape[1]
        best = jnp.broadcast_to(jnp.max(sc, axis=1, keepdims=True), (rows, HEAD))
        if old is not None:
            best = jnp.maximum(old, best)
        p = jnp.exp2(sc - wide(best, n))
        mixed = jnp.dot(p.astype(jnp.bfloat16), v, preferred_element_type=jnp.float32)
        return best, folded(p), mixed

    def head_cols(h):
        return pl.ds(pl.multiple_of(h * HEAD, HEAD), HEAD)

    together = max(n for n in (1, 2, 3, 4, 5) if heads % n == 0)

    for kv in range(2):
        near_copy(kv).wait_recv()

    def early(h):
        x = head_cols(h)
        q = q_ref[:, x]
        sc = jnp.concatenate(
            [scores(q, flat(k_ref[:, :, x])), scores(q, flat(near[0, :, :, x])) + bias_near[...]], axis=1
        )
        top[h], tot[h], acc[h] = weigh(
            sc, jnp.concatenate([flat(v_ref[:, :, x]), flat(near[1, :, :, x])], axis=0)
        )

    def early_step(i, carry):
        for u in range(together):
            early(together * i + u)
        return carry

    lax.fori_loop(0, heads // together, early_step, 0)

    def listed(kv, level, side, n, x, of):
        return jnp.concatenate(
            [stage[kv, of(level, side, j), :, x] for j in range(n)], axis=0
        )

    def mine(level, side, j):
        return lists[0, level, side, j]

    def theirs(level, side, j):
        return lists_got[guest_slot, level, side, j]

    def wait_far(c):
        for i in range(4):
            @pl.when(far_gets[i])
            def _(i=i):
                far_copy(i, c).wait_recv()

    def late(h, u, n_bias, extra):
        x = head_cols(h)
        y = pl.ds(u * HEAD, HEAD)
        k = [flat(far[0, :, :, x]), listed(0, 1, side_in, cap1, y, mine)]
        v = [flat(far[1, :, :, x]), listed(1, 1, side_in, cap1, y, mine)]
        if extra:
            k += [flat(skew[0, :, :, x]), flat(across[0, :, :, x])]
            v += [flat(skew[1, :, :, x]), flat(across[1, :, :, x])]
        sc = scores(q_ref[:, x], jnp.concatenate(k, axis=0)) + bias_late[:, :n_bias]
        old = top[h]
        best, total, mixed = weigh(sc, jnp.concatenate(v, axis=0), old)
        factor = jnp.exp2(old - best)
        return best, tot[h] * factor + total, acc[h] * factor + mixed

    def gate_piece(c):
        passed_copy(c).wait_recv()
        wait_far(c)

        @pl.when(has_out)
        def _():
            skew_copy(c).wait_recv()

        stage[...] = passed[:, :, :, span(c)]
        for u in range(piece):
            h = c * piece + u
            _, total, mixed = late(h, u, bias_late.shape[1], True)
            total = jnp.sum(total, axis=1, keepdims=True)
            out_ref[:, head_cols(h)] = (mixed / total).astype(out_ref.dtype)

    def send_skew(c):
        x = span(c)
        stage[...] = across[:, :, :, x]
        for kv in range(2):
            for j in range(cap1):
                skew_pack[kv, j, :, x] = stage[kv, lists_got[4, 1, side_out, j]]
        skew_copy(c).start()

    pad = bias_guest.shape[1] - rows - half - quarter

    def host(c):
        q_copy(c).wait_recv()
        for u in range(piece):
            h = c * piece + u
            x = head_cols(h)
            y = pl.ds(u * HEAD, HEAD)
            sides = []
            for kv, mine_ref in enumerate((k_ref, v_ref)):
                parts = [flat(across[kv, :, :, x]), listed(kv, 1, side_out, cap1, y, theirs)]
                parts += [mine_ref[theirs(2, side_out, j), :, x] for j in range(cap2)]
                if pad:
                    parts.append(jnp.zeros((pad, HEAD), across.dtype))
                sides.append(jnp.concatenate(parts, axis=0))
            sc = scores(q_got[:, x], sides[0]) + bias_guest[...]
            best, total, mixed = weigh(sc, sides[1])
            total = jnp.broadcast_to(jnp.sum(total, axis=1, keepdims=True), (rows, HEAD))
            o_send[:, x] = (mixed / total).astype(o_send.dtype)
            lse = best + jnp.log2(total)
            lse_send[h] = jnp.transpose(lse)[:8, :]
        o_copy(c).start()
        lse_copy(c).start()

    def outer_piece(c):
        @pl.when(has_in)
        def _():
            send_skew(c)

        passed_copy(c).wait_recv()
        stage[...] = passed[:, :, :, span(c)]

        @pl.when(has_in)
        def _():
            host(c)

        wait_far(c)
        for u in range(piece):
            h = c * piece + u
            top[h], tot[h], acc[h] = late(h, u, far_room + half, False)

    def outer_finish(c):
        @pl.when(has_out)
        def _():
            o_copy(c).wait_recv()
            lse_copy(c).wait_recv()

        for u in range(piece):
            h = c * piece + u
            x = head_cols(h)
            lse = jnp.transpose(jnp.broadcast_to(lse_got[h][:1, :], (HEAD, rows)))
            old = top[h]
            best = jnp.maximum(old, lse)
            factor, guest = jnp.exp2(old - best), jnp.exp2(lse - best)
            total = jnp.sum(tot[h], axis=1, keepdims=True) * factor + guest
            mixed = acc[h] * factor + o_got[:, x].astype(jnp.float32) * guest
            out_ref[:, x] = (mixed / total).astype(out_ref.dtype)

    def turn(c, carry):
        @pl.when(c < pieces)
        def _():
            for kv in range(2):
                across_copy(c, kv).wait_recv()
            passed_copy(c).start()

            @pl.when(outer)
            def _():
                outer_piece(c)

        @pl.when(c > 0)
        def _():
            @pl.when(gate)
            def _():
                gate_piece(c - 1)

            @pl.when(outer)
            def _():
                outer_finish(c - 1)

        return carry

    lax.fori_loop(0, pieces + 1, turn, 0)

    for slot, p, ok in list_sends:
        @pl.when(ok)
        def _(slot=slot, p=p):
            list_copy(slot, p).wait_send()

    for kv in range(2):
        near_copy(kv).wait_send()
    remote(across, across, s_across, r_across.at[0, 0], across_to).wait_send()
    remote(across, passed, s_passed, r_passed.at[0], twin).wait_send()
    for i in range(4):
        @pl.when(far_sends[i])
        def _(i=i):
            r = far_blocks[i]
            remote(
                far_pack.at[:, r], far.at[:, r], s_far.at[i], r_far.at[i, 0], fars[i][0]
            ).wait_send()

    @pl.when(guests)
    def _():
        count_copy().wait_send()
        remote(q_hbm, q_got, s_q, r_q.at[0], d - 4 * s).wait_send()

    @pl.when(hosts)
    def _():
        remote(skew_pack, skew, s_skew, r_skew.at[0], d + 5 * s).wait_send()
        remote(o_send, o_got, s_o, r_o.at[0], d + 4 * s).wait_send()
        remote(lse_send, lse_got, s_lse, r_lse.at[0], d + 4 * s).wait_send()


def shards(n_ctx, queries, keys, values, kv_lists, kv_counts):
    rows, width = queries.shape
    heads = width // HEAD
    nblk = kv_lists.shape[3]
    bs = rows // nblk
    half, quarter = nblk // 2 * bs, nblk // 4 * bs
    far_rows = 2 * (nblk // 4 + nblk // 8) * bs
    far_room = far_rows + (-far_rows) % HEAD
    guest_room = rows + half + quarter
    guest_room += (-guest_room) % HEAD
    piece = PIECE_HEADS if heads % PIECE_HEADS == 0 else 1
    pieces = heads // piece
    kv = jnp.bfloat16
    f32 = jnp.float32
    vmem = pl.BlockSpec(memory_space=pltpu.VMEM)
    hbm = pl.BlockSpec(memory_space=pl.ANY)
    smem = pl.BlockSpec(memory_space=pltpu.SMEM)
    dma = pltpu.SemaphoreType.DMA
    return pl.pallas_call(
        functools.partial(body, n_ctx, nblk, piece),
        out_shape=jax.ShapeDtypeStruct((rows, width), jnp.bfloat16),
        in_specs=[hbm, hbm, hbm, smem, smem],
        out_specs=vmem,
        scratch_shapes=[
            pltpu.VMEM((rows, width), kv),
            pltpu.VMEM((nblk, bs, width), kv),
            pltpu.VMEM((nblk, bs, width), kv),
            pltpu.VMEM((2, nblk, bs, width), kv),
            pltpu.VMEM((2, nblk, bs, width), kv),
            pltpu.VMEM((2, nblk, bs, width), kv),
            pltpu.VMEM((2, half // bs, bs, width), kv),
            pltpu.VMEM((2, half // bs, bs, width), kv),
            pltpu.VMEM((2, far_room // bs, bs, width), kv),
            pltpu.VMEM((2, far_rows // bs, bs, width), kv),
            pltpu.VMEM((2, nblk, bs, piece * HEAD), kv),
            pltpu.VMEM((rows, width), kv),
            pltpu.VMEM((rows, width), kv),
            pltpu.VMEM((rows, width), kv),
            pltpu.VMEM((heads, 8, rows), f32),
            pltpu.VMEM((heads, 8, rows), f32),
            pltpu.VMEM((heads, rows, HEAD), f32),
            pltpu.VMEM((heads, rows, HEAD), f32),
            pltpu.VMEM((heads, rows, HEAD), f32),
            pltpu.VMEM((1, rows), f32),
            pltpu.VMEM((1, far_room + 2 * half + rows), f32),
            pltpu.VMEM((1, guest_room), f32),
            pltpu.SMEM((5,) + kv_lists.shape[1:], jnp.int32),
            pltpu.SMEM((1, kv_counts.shape[2], kv_counts.shape[1]), jnp.int32),
            dma((5,)), dma, dma((2,)), dma, dma, dma, dma((4,)), dma, dma, dma,
            dma((3,)), dma((5,)), dma, dma((2,)), dma((2, pieces)), dma((pieces,)), dma((pieces,)),
            dma((4, pieces)), dma((pieces,)), dma((pieces,)), dma((pieces,)),
        ],
        compiler_params=pltpu.CompilerParams(
            collective_id=0, has_side_effects=True, vmem_limit_bytes=60 * 1024 * 1024
        ),
        name="radial",
    )(
        queries, keys.reshape(nblk, bs, width), values.reshape(nblk, bs, width),
        kv_lists, jnp.swapaxes(kv_counts, 1, 2),
    )


def solution(mesh):
    in_specs = (
        P(("groups", "ctx"), None),
        P(("groups", "ctx"), None),
        P(("groups", "ctx"), None),
        P("ctx", None, None, None),
        P("ctx", None, None),
    )
    out_specs = P(("groups", "ctx"), None)
    return jax.shard_map(
        functools.partial(shards, mesh.shape["ctx"]),
        mesh=mesh, in_specs=in_specs, out_specs=out_specs, check_vma=False,
    )
```

```python
import functools
import math

import jax
import jax.numpy as jnp
from jax import lax
from jax.experimental import pallas as pl
from jax.experimental.pallas import tpu as pltpu
from jax.sharding import PartitionSpec as P

HEAD = 128
MASKED = -1e30
PIECE_HEADS = 2
MESH = pl.DeviceIdType.MESH


def body(
    n_ctx, nblk, piece,
    q_hbm, k_hbm, v_hbm, lists, counts, out_ref,
    q_ref, k_ref, v_ref,
    near, across, passed, skew, skew_pack, far, far_pack, stage,
    q_got, o_send, o_got, lse_send, lse_got,
    acc, top, tot, bias_near, bias_late, bias_guest, lists_got, counts_got,
    s_list, s_count, s_near, s_across, s_passed, s_skew, s_far, s_q, s_o, s_lse,
    r_own, r_list, r_count, r_near, r_across, r_passed, r_skew, r_far, r_q, r_o, r_lse,
):
    own = [
        pltpu.make_async_copy(src, dst, r_own.at[i])
        for i, (src, dst) in enumerate(((k_hbm, k_ref), (v_hbm, v_ref), (q_hbm, q_ref)))
    ]
    for copy in own:
        copy.start()
    rows, width = q_ref.shape
    heads = width // HEAD
    bs = rows // nblk
    cap1, cap2, cap3 = nblk // 2, nblk // 4, nblk // 8
    rate = math.log2(math.e) / math.sqrt(HEAD)
    cols_piece = piece * HEAD
    pieces = heads // piece
    far_room = far.shape[1] * bs

    d = lax.axis_index("ctx")
    place = lax.rem(d, 4)
    quad = d // 4
    quads = n_ctx // 4
    left = place < 2
    s = jnp.where(left, 1, -1)
    gate = (place == 1) | (place == 2)
    outer = jnp.logical_not(gate)
    has_out = jnp.where(left, quad > 0, quad < quads - 1)
    has_in = jnp.where(left, quad < quads - 1, quad > 0)
    side_in = jnp.where(left, 1, 0)
    side_out = 1 - side_in
    twin = jnp.where(gate, d - s, d + s)
    across_to = jnp.where(gate, d + s, d + 3 * s)
    hosts = outer & has_in
    guests = outer & has_out
    gets_skew = gate & has_out

    fars = []
    for distance in (4, 8):
        fars.append((d + distance, d + distance < n_ctx))
        fars.append((d - distance, d - distance >= 0))
    arrives = [fars[1], fars[0], fars[3], fars[2]]
    far_rows = (cap2 * bs, cap2 * bs, cap3 * bs, cap3 * bs)
    far_start = (0, cap2 * bs, 2 * cap2 * bs, (2 * cap2 + cap3) * bs)
    far_blocks = [pl.ds(a // bs, n // bs) for a, n in zip(far_start, far_rows)]
    hosted = (outer & left, outer & jnp.logical_not(left), jnp.bool_(False), jnp.bool_(False))
    far_sends = [ok & jnp.logical_not(hosted[i]) for i, (_, ok) in enumerate(fars)]
    far_gets = [ok & jnp.logical_not(hosted[i]) for i, (_, ok) in enumerate(arrives)]
    guest_slot = jnp.where(left, 0, 1)

    def to(device):
        return {"ctx": device}

    barrier = pltpu.get_barrier_semaphore()
    always = jnp.bool_(True)
    partners = [(p, ok) for p, ok in fars]
    partners += [
        (twin, always),
        (across_to, always),
        (d + 5 * s, hosts),
        (d - 5 * s, gets_skew),
    ]
    count = jnp.int32(0)
    for p, ok in partners:
        count = count + ok.astype(jnp.int32)

        @pl.when(ok)
        def _(p=p):
            pl.semaphore_signal(barrier, inc=1, device_id=to(p), device_id_type=MESH)

    pl.semaphore_wait(barrier, count)

    def remote(src, dst, ssem, rsem, device):
        return pltpu.make_async_remote_copy(
            src_ref=src, dst_ref=dst, send_sem=ssem, recv_sem=rsem,
            device_id=to(device), device_id_type=MESH,
        )

    def span(c):
        return pl.ds(pl.multiple_of(c * cols_piece, cols_piece), cols_piece)

    flip = (1, 0, 3, 2)

    def list_copy(slot, device):
        return remote(lists.at[0], lists_got.at[slot], s_list.at[slot], r_list.at[slot], device)

    def count_copy():
        return remote(counts, counts_got, s_count, r_count, d - 4 * s)

    def near_copy(kv):
        return remote((k_hbm, v_hbm)[kv], near.at[kv], s_near.at[kv], r_near.at[kv], twin)

    def across_copy(c, kv):
        x = span(c)
        return remote(
            (k_hbm, v_hbm)[kv].at[:, :, x], across.at[kv, :, :, x], s_across, r_across.at[kv, c], across_to
        )

    def passed_copy(c):
        x = span(c)
        return remote(across.at[:, :, :, x], passed.at[:, :, :, x], s_passed, r_passed.at[c], twin)

    def skew_copy(c):
        x = span(c)
        return remote(skew_pack.at[:, :, :, x], skew.at[:, :, :, x], s_skew, r_skew.at[c], d + 5 * s)

    def far_copy(i, c):
        r, x = far_blocks[i], span(c)
        return remote(
            far_pack.at[:, r, :, x], far.at[:, r, :, x], s_far.at[i], r_far.at[i, c], fars[i][0]
        )

    def q_copy(c):
        x = span(c)
        return remote(q_hbm.at[:, x], q_got.at[:, x], s_q, r_q.at[c], d - 4 * s)

    def o_copy(c):
        x = span(c)
        return remote(o_send.at[:, x], o_got.at[:, x], s_o, r_o.at[c], d + 4 * s)

    def lse_copy(c):
        h = pl.ds(c * piece, piece)
        return remote(lse_send.at[h], lse_got.at[h], s_lse, r_lse.at[c], d + 4 * s)

    def each_piece(one):
        def step(c, carry):
            one(c)
            return carry

        lax.fori_loop(0, pieces, step, 0)

    list_sends = [(flip[i], p, ok) for i, (p, ok) in enumerate(fars)] + [(4, d - 5 * s, gets_skew)]
    list_gets = [(i, p, ok) for i, (p, ok) in enumerate(fars)] + [(4, d + 5 * s, hosts)]
    for slot, p, ok in list_sends:
        @pl.when(ok)
        def _(slot=slot, p=p):
            list_copy(slot, p).start()

    @pl.when(guests)
    def _():
        count_copy().start()

    def start_across(c):
        for kv in range(2):
            across_copy(c, kv).start()

    each_piece(start_across)
    for kv in range(2):
        near_copy(kv).start()

    for i in range(4):
        @pl.when(jnp.logical_not(far_gets[i]))
        def _(i=i):
            for kv in range(2):
                far[kv, far_blocks[i]] = jnp.zeros((far_rows[i] // bs, bs, width), far.dtype)

    spare = far_room - sum(far_rows)
    if spare:
        for kv in range(2):
            far[kv, pl.ds(sum(far_rows) // bs, spare // bs)] = jnp.zeros(
                (spare // bs, bs, width), far.dtype
            )

    @pl.when(gate & jnp.logical_not(has_out))
    def _():
        for kv in range(2):
            skew[kv] = jnp.zeros(skew.shape[1:], skew.dtype)

    @pl.when(outer & jnp.logical_not(has_out))
    def _():
        o_got[...] = jnp.zeros(o_got.shape, o_got.dtype)
        lse_got[...] = jnp.full(lse_got.shape, MASKED, lse_got.dtype)

    for copy in own:
        copy.wait()

    def flat(x):
        return x.reshape(x.shape[0] * x.shape[1], x.shape[2])

    for i, p, ok in list_gets:
        @pl.when(ok)
        def _(i=i, p=p):
            list_copy(i, p).wait_recv()
            if i < 4:
                for j in range(far_rows[i] // bs):
                    source = lists_got[i, 2 + i // 2, i % 2, j]
                    far_pack[0, far_start[i] // bs + j] = k_ref[source]
                    far_pack[1, far_start[i] // bs + j] = v_ref[source]

    @pl.when(hosts)
    def _():
        count_copy().wait_recv()

    def start_far(c):
        @pl.when(guests)
        def _():
            q_copy(c).start()

        for i in range(4):
            @pl.when(far_sends[i])
            def _(i=i):
                far_copy(i, c).start()

    each_piece(start_far)

    def as_bias(seen):
        return jnp.where(seen, 0.0, MASKED).astype(jnp.float32)

    def full_bias(listed, counted):
        block = lax.broadcasted_iota(jnp.int32, (1, rows), 1) // bs
        seen = jnp.zeros((1, rows), jnp.int32)
        for j in range(nblk):
            hit = (block == listed(j)) & (jnp.full((1, rows), j) < counted)
            seen = seen + hit.astype(jnp.int32)
        return as_bias(seen > 0)

    def listed_bias(n, counted):
        column = lax.broadcasted_iota(jnp.int32, (1, n), 1)
        return as_bias(column < counted * bs)

    half = cap1 * bs
    quarter = cap2 * bs
    side_near = jnp.where(gate, side_out, side_in)
    bias_near[...] = full_bias(lambda j: lists[0, 0, side_near, j], counts[0, side_near, 0])
    column = lax.broadcasted_iota(jnp.int32, (1, far_room), 1)
    limit = jnp.zeros(column.shape, jnp.int32)
    for i in range(4):
        shown = jnp.where(far_gets[i], counts[0, i % 2, 2 + i // 2], 0)
        limit = jnp.where(column >= far_start[i], far_start[i] + shown * bs, limit)
    limit = jnp.where(column >= sum(far_rows), 0, limit)
    bias_late[:, :far_room] = as_bias(column < limit)
    bias_late[:, far_room:far_room + half] = listed_bias(half, counts[0, side_in, 1])
    bias_late[:, far_room + half:far_room + 2 * half] = listed_bias(half, counts[0, side_out, 1])
    bias_late[:, far_room + 2 * half:] = full_bias(
        lambda j: lists[0, 0, side_in, j], counts[0, side_in, 0]
    )

    @pl.when(hosts)
    def _():
        bias_guest[:, :rows] = full_bias(
            lambda j: lists_got[guest_slot, 0, side_out, j], counts_got[0, side_out, 0]
        )
        bias_guest[:, rows:rows + half] = listed_bias(half, counts_got[0, side_out, 1])
        bias_guest[:, rows + half:] = listed_bias(
            bias_guest.shape[1] - rows - half, counts_got[0, side_out, 2]
        )

    def wide(x, n):
        return jnp.concatenate([x] * (n // HEAD), axis=1)

    def folded(p):
        total = p[:, :HEAD]
        for i in range(1, p.shape[1] // HEAD):
            total = total + p[:, i * HEAD:(i + 1) * HEAD]
        return total

    def scores(q, k):
        return lax.dot_general(
            q, k, (((1,), (1,)), ((), ())), preferred_element_type=jnp.float32
        ) * rate

    def weigh(sc, v, old=None):
        n = sc.shape[1]
        best = jnp.broadcast_to(jnp.max(sc, axis=1, keepdims=True), (rows, HEAD))
        if old is not None:
            best = jnp.maximum(old, best)
        p = jnp.exp2(sc - wide(best, n))
        mixed = jnp.dot(p.astype(jnp.bfloat16), v, preferred_element_type=jnp.float32)
        return best, folded(p), mixed

    def head_cols(h):
        return pl.ds(pl.multiple_of(h * HEAD, HEAD), HEAD)

    together = max(n for n in (1, 2, 3, 4, 5) if heads % n == 0)

    for kv in range(2):
        near_copy(kv).wait_recv()

    def early(h):
        x = head_cols(h)
        q = q_ref[:, x]
        sc = jnp.concatenate(
            [scores(q, flat(k_ref[:, :, x])), scores(q, flat(near[0, :, :, x])) + bias_near[...]], axis=1
        )
        top[h], tot[h], acc[h] = weigh(
            sc, jnp.concatenate([flat(v_ref[:, :, x]), flat(near[1, :, :, x])], axis=0)
        )

    def early_step(i, carry):
        for u in range(together):
            early(together * i + u)
        return carry

    lax.fori_loop(0, heads // together, early_step, 0)

    def listed(kv, level, side, n, x, of):
        return jnp.concatenate(
            [stage[kv, of(level, side, j), :, x] for j in range(n)], axis=0
        )

    def mine(level, side, j):
        return lists[0, level, side, j]

    def theirs(level, side, j):
        return lists_got[guest_slot, level, side, j]

    def wait_far(c):
        for i in range(4):
            @pl.when(far_gets[i])
            def _(i=i):
                far_copy(i, c).wait_recv()

    def late(h, u, n_bias, extra):
        x = head_cols(h)
        y = pl.ds(u * HEAD, HEAD)
        k = [flat(far[0, :, :, x]), listed(0, 1, side_in, cap1, y, mine)]
        v = [flat(far[1, :, :, x]), listed(1, 1, side_in, cap1, y, mine)]
        if extra:
            k += [flat(skew[0, :, :, x]), flat(across[0, :, :, x])]
            v += [flat(skew[1, :, :, x]), flat(across[1, :, :, x])]
        sc = scores(q_ref[:, x], jnp.concatenate(k, axis=0)) + bias_late[:, :n_bias]
        old = top[h]
        best, total, mixed = weigh(sc, jnp.concatenate(v, axis=0), old)
        factor = jnp.exp2(old - best)
        return best, tot[h] * factor + total, acc[h] * factor + mixed

    def gate_piece(c):
        passed_copy(c).wait_recv()
        wait_far(c)

        @pl.when(has_out)
        def _():
            skew_copy(c).wait_recv()

        stage[...] = passed[:, :, :, span(c)]
        for u in range(piece):
            h = c * piece + u
            _, total, mixed = late(h, u, bias_late.shape[1], True)
            total = jnp.sum(total, axis=1, keepdims=True)
            out_ref[:, head_cols(h)] = (mixed / total).astype(out_ref.dtype)

    def send_skew(c):
        x = span(c)
        stage[...] = across[:, :, :, x]
        for kv in range(2):
            for j in range(cap1):
                skew_pack[kv, j, :, x] = stage[kv, lists_got[4, 1, side_out, j]]
        skew_copy(c).start()

    pad = bias_guest.shape[1] - rows - half - quarter

    def host(c):
        q_copy(c).wait_recv()
        for u in range(piece):
            h = c * piece + u
            x = head_cols(h)
            y = pl.ds(u * HEAD, HEAD)
            sides = []
            for kv, mine_ref in enumerate((k_ref, v_ref)):
                parts = [flat(across[kv, :, :, x]), listed(kv, 1, side_out, cap1, y, theirs)]
                parts += [mine_ref[theirs(2, side_out, j), :, x] for j in range(cap2)]
                if pad:
                    parts.append(jnp.zeros((pad, HEAD), across.dtype))
                sides.append(jnp.concatenate(parts, axis=0))
            sc = scores(q_got[:, x], sides[0]) + bias_guest[...]
            best, total, mixed = weigh(sc, sides[1])
            total = jnp.broadcast_to(jnp.sum(total, axis=1, keepdims=True), (rows, HEAD))
            o_send[:, x] = (mixed / total).astype(o_send.dtype)
            lse = best + jnp.log2(total)
            lse_send[h] = jnp.transpose(lse)[:8, :]
        o_copy(c).start()
        lse_copy(c).start()

    def outer_piece(c):
        @pl.when(has_in)
        def _():
            send_skew(c)

        passed_copy(c).wait_recv()
        stage[...] = passed[:, :, :, span(c)]

        @pl.when(has_in)
        def _():
            host(c)

        wait_far(c)
        for u in range(piece):
            h = c * piece + u
            top[h], tot[h], acc[h] = late(h, u, far_room + half, False)

    def outer_finish(c):
        @pl.when(has_out)
        def _():
            o_copy(c).wait_recv()
            lse_copy(c).wait_recv()

        for u in range(piece):
            h = c * piece + u
            x = head_cols(h)
            lse = jnp.transpose(jnp.broadcast_to(lse_got[h][:1, :], (HEAD, rows)))
            old = top[h]
            best = jnp.maximum(old, lse)
            factor, guest = jnp.exp2(old - best), jnp.exp2(lse - best)
            total = jnp.sum(tot[h], axis=1, keepdims=True) * factor + guest
            mixed = acc[h] * factor + o_got[:, x].astype(jnp.float32) * guest
            out_ref[:, x] = (mixed / total).astype(out_ref.dtype)

    def turn(c, carry):
        @pl.when(c < pieces)
        def _():
            for kv in range(2):
                across_copy(c, kv).wait_recv()
            passed_copy(c).start()

            @pl.when(outer)
            def _():
                outer_piece(c)

        @pl.when(c > 0)
        def _():
            @pl.when(gate)
            def _():
                gate_piece(c - 1)

            @pl.when(outer)
            def _():
                outer_finish(c - 1)

        return carry

    lax.fori_loop(0, pieces + 1, turn, 0)

    for slot, p, ok in list_sends:
        @pl.when(ok)
        def _(slot=slot, p=p):
            list_copy(slot, p).wait_send()

    for kv in range(2):
        near_copy(kv).wait_send()
    remote(across, across, s_across, r_across.at[0, 0], across_to).wait_send()
    remote(across, passed, s_passed, r_passed.at[0], twin).wait_send()
    for i in range(4):
        @pl.when(far_sends[i])
        def _(i=i):
            r = far_blocks[i]
            remote(
                far_pack.at[:, r], far.at[:, r], s_far.at[i], r_far.at[i, 0], fars[i][0]
            ).wait_send()

    @pl.when(guests)
    def _():
        count_copy().wait_send()
        remote(q_hbm, q_got, s_q, r_q.at[0], d - 4 * s).wait_send()

    @pl.when(hosts)
    def _():
        remote(skew_pack, skew, s_skew, r_skew.at[0], d + 5 * s).wait_send()
        remote(o_send, o_got, s_o, r_o.at[0], d + 4 * s).wait_send()
        remote(lse_send, lse_got, s_lse, r_lse.at[0], d + 4 * s).wait_send()


def shards(n_ctx, queries, keys, values, kv_lists, kv_counts):
    rows, width = queries.shape
    heads = width // HEAD
    nblk = kv_lists.shape[3]
    bs = rows // nblk
    half, quarter = nblk // 2 * bs, nblk // 4 * bs
    far_rows = 2 * (nblk // 4 + nblk // 8) * bs
    far_room = far_rows + (-far_rows) % HEAD
    guest_room = rows + half + quarter
    guest_room += (-guest_room) % HEAD
    piece = PIECE_HEADS if heads % PIECE_HEADS == 0 else 1
    pieces = heads // piece
    kv = jnp.bfloat16
    f32 = jnp.float32
    vmem = pl.BlockSpec(memory_space=pltpu.VMEM)
    hbm = pl.BlockSpec(memory_space=pl.ANY)
    smem = pl.BlockSpec(memory_space=pltpu.SMEM)
    dma = pltpu.SemaphoreType.DMA
    return pl.pallas_call(
        functools.partial(body, n_ctx, nblk, piece),
        out_shape=pltpu.VMEM((rows, width), jnp.bfloat16),
        in_specs=[hbm, hbm, hbm, smem, smem],
        out_specs=vmem,
        scratch_shapes=[
            pltpu.VMEM((rows, width), kv),
            pltpu.VMEM((nblk, bs, width), kv),
            pltpu.VMEM((nblk, bs, width), kv),
            pltpu.VMEM((2, nblk, bs, width), kv),
            pltpu.VMEM((2, nblk, bs, width), kv),
            pltpu.VMEM((2, nblk, bs, width), kv),
            pltpu.VMEM((2, half // bs, bs, width), kv),
            pltpu.VMEM((2, half // bs, bs, width), kv),
            pltpu.VMEM((2, far_room // bs, bs, width), kv),
            pltpu.VMEM((2, far_rows // bs, bs, width), kv),
            pltpu.VMEM((2, nblk, bs, piece * HEAD), kv),
            pltpu.VMEM((rows, width), kv),
            pltpu.VMEM((rows, width), kv),
            pltpu.VMEM((rows, width), kv),
            pltpu.VMEM((heads, 8, rows), f32),
            pltpu.VMEM((heads, 8, rows), f32),
            pltpu.VMEM((heads, rows, HEAD), f32),
            pltpu.VMEM((heads, rows, HEAD), f32),
            pltpu.VMEM((heads, rows, HEAD), f32),
            pltpu.VMEM((1, rows), f32),
            pltpu.VMEM((1, far_room + 2 * half + rows), f32),
            pltpu.VMEM((1, guest_room), f32),
            pltpu.SMEM((5,) + kv_lists.shape[1:], jnp.int32),
            pltpu.SMEM((1, kv_counts.shape[2], kv_counts.shape[1]), jnp.int32),
            dma((5,)), dma, dma((2,)), dma, dma, dma, dma((4,)), dma, dma, dma,
            dma((3,)), dma((5,)), dma, dma((2,)), dma((2, pieces)), dma((pieces,)), dma((pieces,)),
            dma((4, pieces)), dma((pieces,)), dma((pieces,)), dma((pieces,)),
        ],
        compiler_params=pltpu.CompilerParams(
            collective_id=0, has_side_effects=True, vmem_limit_bytes=60 * 1024 * 1024
        ),
        name="radial",
    )(
        queries, keys.reshape(nblk, bs, width), values.reshape(nblk, bs, width),
        kv_lists, jnp.swapaxes(kv_counts, 1, 2),
    )


def solution(mesh):
    in_specs = (
        P(("groups", "ctx"), None),
        P(("groups", "ctx"), None),
        P(("groups", "ctx"), None),
        P("ctx", None, None, None),
        P("ctx", None, None),
    )
    out_specs = P(("groups", "ctx"), None)
    return jax.shard_map(
        functools.partial(shards, mesh.shape["ctx"]),
        mesh=mesh, in_specs=in_specs, out_specs=out_specs, check_vma=False,
    )
```

```python
import functools
import math

import jax
import jax.numpy as jnp
from jax import lax
from jax.experimental import pallas as pl
from jax.experimental.pallas import tpu as pltpu
from jax.sharding import PartitionSpec as P

HEAD = 128
MASKED = -1e30
PIECE_HEADS = 1
MESH = pl.DeviceIdType.MESH


def body(
    n_ctx, nblk, piece,
    q_hbm, k_hbm, v_hbm, lists, counts, out_ref,
    q_ref, k_ref, v_ref,
    near, across, passed, skew, skew_pack, far, far_pack, stage,
    q_got, o_send, o_got, lse_send, lse_got,
    acc, top, tot, bias_near, bias_late, bias_guest, lists_got, counts_got, ready,
    s_list, s_count, s_near, s_across, s_passed, s_skew, s_far, s_q, s_o, s_lse,
    r_own, r_list, r_count, r_near, r_across, r_passed, r_skew, r_far, r_q, r_o, r_lse,
):
    own = [
        pltpu.make_async_copy(src, dst, r_own.at[i])
        for i, (src, dst) in enumerate(((k_hbm, k_ref), (v_hbm, v_ref), (q_hbm, q_ref)))
    ]
    for copy in own:
        copy.start()
    rows, width = q_ref.shape
    heads = width // HEAD
    bs = rows // nblk
    cap1, cap2, cap3 = nblk // 2, nblk // 4, nblk // 8
    rate = math.log2(math.e) / math.sqrt(HEAD)
    cols_piece = piece * HEAD
    pieces = heads // piece
    far_room = far.shape[1] * bs

    d = lax.axis_index("ctx")
    place = lax.rem(d, 4)
    quad = d // 4
    quads = n_ctx // 4
    left = place < 2
    s = jnp.where(left, 1, -1)
    gate = (place == 1) | (place == 2)
    outer = jnp.logical_not(gate)
    has_out = jnp.where(left, quad > 0, quad < quads - 1)
    has_in = jnp.where(left, quad < quads - 1, quad > 0)
    side_in = jnp.where(left, 1, 0)
    side_out = 1 - side_in
    twin = jnp.where(gate, d - s, d + s)
    across_to = jnp.where(gate, d + s, d + 3 * s)
    hosts = outer & has_in
    guests = outer & has_out
    gets_skew = gate & has_out

    fars = []
    for distance in (4, 8):
        fars.append((d + distance, d + distance < n_ctx))
        fars.append((d - distance, d - distance >= 0))
    arrives = [fars[1], fars[0], fars[3], fars[2]]
    far_rows = (cap2 * bs, cap2 * bs, cap3 * bs, cap3 * bs)
    far_start = (0, cap2 * bs, 2 * cap2 * bs, (2 * cap2 + cap3) * bs)
    far_blocks = [pl.ds(a // bs, n // bs) for a, n in zip(far_start, far_rows)]
    hosted = (outer & left, outer & jnp.logical_not(left), jnp.bool_(False), jnp.bool_(False))
    far_sends = [ok & jnp.logical_not(hosted[i]) for i, (_, ok) in enumerate(fars)]
    far_gets = [ok & jnp.logical_not(hosted[i]) for i, (_, ok) in enumerate(arrives)]
    guest_slot = jnp.where(left, 0, 1)

    def to(device):
        return {"ctx": device}

    barrier = pltpu.get_barrier_semaphore()
    always = jnp.bool_(True)
    partners = [(p, ok) for p, ok in fars[:2]]
    partners += [
        (twin, always),
        (across_to, always),
        (d + 5 * s, hosts),
        (d - 5 * s, gets_skew),
    ]
    count = jnp.int32(0)
    for p, ok in partners:
        count = count + ok.astype(jnp.int32)

        @pl.when(ok)
        def _(p=p):
            pl.semaphore_signal(barrier, inc=1, device_id=to(p), device_id_type=MESH)

    pl.semaphore_wait(barrier, count)

    @pl.when(fars[0][1] & fars[1][1])
    def _():
        for i in range(2):
            pl.semaphore_signal(
                ready.at[1 - i], inc=1, device_id=to(fars[i][0]), device_id_type=MESH
            )

    def remote(src, dst, ssem, rsem, device):
        return pltpu.make_async_remote_copy(
            src_ref=src, dst_ref=dst, send_sem=ssem, recv_sem=rsem,
            device_id=to(device), device_id_type=MESH,
        )

    def span(c):
        return pl.ds(pl.multiple_of(c * cols_piece, cols_piece), cols_piece)

    flip = (1, 0, 3, 2)

    def list_copy(slot, device):
        return remote(lists.at[0], lists_got.at[slot], s_list.at[slot], r_list.at[slot], device)

    def count_copy():
        return remote(counts, counts_got, s_count, r_count, d - 4 * s)

    def near_copy(kv):
        return remote((k_hbm, v_hbm)[kv], near.at[kv], s_near.at[kv], r_near.at[kv], twin)

    def across_copy(c, kv):
        x = span(c)
        return remote(
            (k_hbm, v_hbm)[kv].at[:, :, x], across.at[kv, :, :, x], s_across, r_across.at[kv, c], across_to
        )

    def passed_copy(c):
        x = span(c)
        return remote(across.at[:, :, :, x], passed.at[:, :, :, x], s_passed, r_passed.at[c], twin)

    def skew_copy(c):
        x = span(c)
        return remote(skew_pack.at[:, :, :, x], skew.at[:, :, :, x], s_skew, r_skew.at[c], d + 5 * s)

    def far_copy(i, c):
        r, x = far_blocks[i], span(c)
        return remote(
            far_pack.at[:, r, :, x], far.at[:, r, :, x], s_far.at[i], r_far.at[i, c], fars[i][0]
        )

    def q_copy(c):
        x = span(c)
        return remote(q_hbm.at[:, x], q_got.at[:, x], s_q, r_q.at[c], d - 4 * s)

    def o_copy(c):
        x = span(c)
        return remote(o_send.at[:, x], o_got.at[:, x], s_o, r_o.at[c], d + 4 * s)

    def lse_copy(c):
        h = pl.ds(c * piece, piece)
        return remote(lse_send.at[h], lse_got.at[h], s_lse, r_lse.at[c], d + 4 * s)

    def each_piece(one):
        def step(c, carry):
            one(c)
            return carry

        lax.fori_loop(0, pieces, step, 0)

    list_sends = [(flip[i], p, ok) for i, (p, ok) in enumerate(fars)] + [(4, d - 5 * s, gets_skew)]
    list_gets = [(i, p, ok) for i, (p, ok) in enumerate(fars)] + [(4, d + 5 * s, hosts)]
    for slot, p, ok in list_sends:
        if slot not in (2, 3):
            @pl.when(ok)
            def _(slot=slot, p=p):
                list_copy(slot, p).start()

    @pl.when(guests)
    def _():
        count_copy().start()

    def start_across(c):
        for kv in range(2):
            across_copy(c, kv).start()

    each_piece(start_across)
    for kv in range(2):
        near_copy(kv).start()

    for i in range(2):
        @pl.when(fars[2 + i][1])
        def _(i=i):
            pl.semaphore_wait(ready.at[i], 1)
            list_copy(flip[2 + i], fars[2 + i][0]).start()

    for i in range(4):
        @pl.when(jnp.logical_not(far_gets[i]))
        def _(i=i):
            for kv in range(2):
                far[kv, far_blocks[i]] = jnp.zeros((far_rows[i] // bs, bs, width), far.dtype)

    spare = far_room - sum(far_rows)
    if spare:
        for kv in range(2):
            far[kv, pl.ds(sum(far_rows) // bs, spare // bs)] = jnp.zeros(
                (spare // bs, bs, width), far.dtype
            )

    @pl.when(gate & jnp.logical_not(has_out))
    def _():
        for kv in range(2):
            skew[kv] = jnp.zeros(skew.shape[1:], skew.dtype)

    @pl.when(outer & jnp.logical_not(has_out))
    def _():
        o_got[...] = jnp.zeros(o_got.shape, o_got.dtype)
        lse_got[...] = jnp.full(lse_got.shape, MASKED, lse_got.dtype)

    for copy in own:
        copy.wait()

    def flat(x):
        return x.reshape(x.shape[0] * x.shape[1], x.shape[2])

    for i, p, ok in list_gets:
        @pl.when(ok)
        def _(i=i, p=p):
            list_copy(i, p).wait_recv()
            if i < 4:
                for j in range(far_rows[i] // bs):
                    source = lists_got[i, 2 + i // 2, i % 2, j]
                    far_pack[0, far_start[i] // bs + j] = k_ref[source]
                    far_pack[1, far_start[i] // bs + j] = v_ref[source]

    @pl.when(hosts)
    def _():
        count_copy().wait_recv()

    def start_far(c):
        @pl.when(guests)
        def _():
            q_copy(c).start()

        for i in range(4):
            @pl.when(far_sends[i])
            def _(i=i):
                far_copy(i, c).start()

    each_piece(start_far)

    def as_bias(seen):
        return jnp.where(seen, 0.0, MASKED).astype(jnp.float32)

    def full_bias(listed, counted):
        block = lax.broadcasted_iota(jnp.int32, (1, rows), 1) // bs
        seen = jnp.zeros((1, rows), jnp.int32)
        for j in range(nblk):
            hit = (block == listed(j)) & (jnp.full((1, rows), j) < counted)
            seen = seen + hit.astype(jnp.int32)
        return as_bias(seen > 0)

    def listed_bias(n, counted):
        column = lax.broadcasted_iota(jnp.int32, (1, n), 1)
        return as_bias(column < counted * bs)

    half = cap1 * bs
    quarter = cap2 * bs
    side_near = jnp.where(gate, side_out, side_in)
    bias_near[...] = full_bias(lambda j: lists[0, 0, side_near, j], counts[0, side_near, 0])
    column = lax.broadcasted_iota(jnp.int32, (1, far_room), 1)
    limit = jnp.zeros(column.shape, jnp.int32)
    for i in range(4):
        shown = jnp.where(far_gets[i], counts[0, i % 2, 2 + i // 2], 0)
        limit = jnp.where(column >= far_start[i], far_start[i] + shown * bs, limit)
    limit = jnp.where(column >= sum(far_rows), 0, limit)
    bias_late[:, :far_room] = as_bias(column < limit)
    bias_late[:, far_room:far_room + half] = listed_bias(half, counts[0, side_in, 1])
    bias_late[:, far_room + half:far_room + 2 * half] = listed_bias(half, counts[0, side_out, 1])
    bias_late[:, far_room + 2 * half:] = full_bias(
        lambda j: lists[0, 0, side_in, j], counts[0, side_in, 0]
    )

    @pl.when(hosts)
    def _():
        bias_guest[:, :rows] = full_bias(
            lambda j: lists_got[guest_slot, 0, side_out, j], counts_got[0, side_out, 0]
        )
        bias_guest[:, rows:rows + half] = listed_bias(half, counts_got[0, side_out, 1])
        bias_guest[:, rows + half:] = listed_bias(
            bias_guest.shape[1] - rows - half, counts_got[0, side_out, 2]
        )

    def wide(x, n):
        return jnp.concatenate([x] * (n // HEAD), axis=1)

    def folded(p):
        total = p[:, :HEAD]
        for i in range(1, p.shape[1] // HEAD):
            total = total + p[:, i * HEAD:(i + 1) * HEAD]
        return total

    def scores(q, k):
        return lax.dot_general(
            q, k, (((1,), (1,)), ((), ())), preferred_element_type=jnp.float32
        ) * rate

    def weigh(sc, v, old=None):
        n = sc.shape[1]
        best = jnp.broadcast_to(jnp.max(sc, axis=1, keepdims=True), (rows, HEAD))
        if old is not None:
            best = jnp.maximum(old, best)
        p = jnp.exp2(sc - wide(best, n))
        mixed = jnp.dot(p.astype(jnp.bfloat16), v, preferred_element_type=jnp.float32)
        return best, folded(p), mixed

    def head_cols(h):
        return pl.ds(pl.multiple_of(h * HEAD, HEAD), HEAD)

    together = max(n for n in (1, 2, 3, 4, 5) if heads % n == 0)

    for kv in range(2):
        near_copy(kv).wait_recv()

    def early(h):
        x = head_cols(h)
        q = q_ref[:, x]
        sc = jnp.concatenate(
            [scores(q, flat(k_ref[:, :, x])), scores(q, flat(near[0, :, :, x])) + bias_near[...]], axis=1
        )
        top[h], tot[h], acc[h] = weigh(
            sc, jnp.concatenate([flat(v_ref[:, :, x]), flat(near[1, :, :, x])], axis=0)
        )

    def early_step(i, carry):
        for u in range(together):
            early(together * i + u)
        return carry

    lax.fori_loop(0, heads // together, early_step, 0)

    def listed(kv, level, side, n, x, of):
        return jnp.concatenate(
            [stage[kv, of(level, side, j), :, x] for j in range(n)], axis=0
        )

    def mine(level, side, j):
        return lists[0, level, side, j]

    def theirs(level, side, j):
        return lists_got[guest_slot, level, side, j]

    def wait_far(c):
        for i in range(4):
            @pl.when(far_gets[i])
            def _(i=i):
                far_copy(i, c).wait_recv()

    def late(h, u, n_bias, extra):
        x = head_cols(h)
        y = pl.ds(u * HEAD, HEAD)
        k = [flat(far[0, :, :, x]), listed(0, 1, side_in, cap1, y, mine)]
        v = [flat(far[1, :, :, x]), listed(1, 1, side_in, cap1, y, mine)]
        if extra:
            k += [flat(skew[0, :, :, x]), flat(across[0, :, :, x])]
            v += [flat(skew[1, :, :, x]), flat(across[1, :, :, x])]
        sc = scores(q_ref[:, x], jnp.concatenate(k, axis=0)) + bias_late[:, :n_bias]
        old = top[h]
        best, total, mixed = weigh(sc, jnp.concatenate(v, axis=0), old)
        factor = jnp.exp2(old - best)
        return best, tot[h] * factor + total, acc[h] * factor + mixed

    def gate_piece(c):
        passed_copy(c).wait_recv()
        wait_far(c)

        @pl.when(has_out)
        def _():
            skew_copy(c).wait_recv()

        stage[...] = passed[:, :, :, span(c)]
        for u in range(piece):
            h = c * piece + u
            _, total, mixed = late(h, u, bias_late.shape[1], True)
            total = jnp.sum(total, axis=1, keepdims=True)
            out_ref[:, head_cols(h)] = (mixed / total).astype(out_ref.dtype)

    def send_skew(c):
        x = span(c)
        stage[...] = across[:, :, :, x]
        for kv in range(2):
            for j in range(cap1):
                skew_pack[kv, j, :, x] = stage[kv, lists_got[4, 1, side_out, j]]
        skew_copy(c).start()

    pad = bias_guest.shape[1] - rows - half - quarter

    def host(c):
        q_copy(c).wait_recv()
        for u in range(piece):
            h = c * piece + u
            x = head_cols(h)
            y = pl.ds(u * HEAD, HEAD)
            sides = []
            for kv, mine_ref in enumerate((k_ref, v_ref)):
                parts = [flat(across[kv, :, :, x]), listed(kv, 1, side_out, cap1, y, theirs)]
                parts += [mine_ref[theirs(2, side_out, j), :, x] for j in range(cap2)]
                if pad:
                    parts.append(jnp.zeros((pad, HEAD), across.dtype))
                sides.append(jnp.concatenate(parts, axis=0))
            sc = scores(q_got[:, x], sides[0]) + bias_guest[...]
            best, total, mixed = weigh(sc, sides[1])
            total = jnp.broadcast_to(jnp.sum(total, axis=1, keepdims=True), (rows, HEAD))
            o_send[:, x] = (mixed / total).astype(o_send.dtype)
            lse = best + jnp.log2(total)
            lse_send[h] = jnp.transpose(lse)[:8, :]
        o_copy(c).start()
        lse_copy(c).start()

    def outer_piece(c):
        @pl.when(has_in)
        def _():
            send_skew(c)

        passed_copy(c).wait_recv()
        stage[...] = passed[:, :, :, span(c)]

        @pl.when(has_in)
        def _():
            host(c)

        wait_far(c)
        for u in range(piece):
            h = c * piece + u
            top[h], tot[h], acc[h] = late(h, u, far_room + half, False)

    def outer_finish(c):
        @pl.when(has_out)
        def _():
            o_copy(c).wait_recv()
            lse_copy(c).wait_recv()

        for u in range(piece):
            h = c * piece + u
            x = head_cols(h)
            lse = jnp.transpose(jnp.broadcast_to(lse_got[h][:1, :], (HEAD, rows)))
            old = top[h]
            best = jnp.maximum(old, lse)
            factor, guest = jnp.exp2(old - best), jnp.exp2(lse - best)
            total = jnp.sum(tot[h], axis=1, keepdims=True) * factor + guest
            mixed = acc[h] * factor + o_got[:, x].astype(jnp.float32) * guest
            out_ref[:, x] = (mixed / total).astype(out_ref.dtype)

    def turn(c, carry):
        @pl.when(c < pieces)
        def _():
            for kv in range(2):
                across_copy(c, kv).wait_recv()
            passed_copy(c).start()

            @pl.when(outer)
            def _():
                outer_piece(c)

        @pl.when(c > 0)
        def _():
            @pl.when(gate)
            def _():
                gate_piece(c - 1)

            @pl.when(outer)
            def _():
                outer_finish(c - 1)

        return carry

    lax.fori_loop(0, pieces + 1, turn, 0)

    for slot, p, ok in list_sends:
        @pl.when(ok)
        def _(slot=slot, p=p):
            list_copy(slot, p).wait_send()

    for kv in range(2):
        near_copy(kv).wait_send()
    remote(across, across, s_across, r_across.at[0, 0], across_to).wait_send()
    remote(across, passed, s_passed, r_passed.at[0], twin).wait_send()
    for i in range(4):
        @pl.when(far_sends[i])
        def _(i=i):
            r = far_blocks[i]
            remote(
                far_pack.at[:, r], far.at[:, r], s_far.at[i], r_far.at[i, 0], fars[i][0]
            ).wait_send()

    @pl.when(guests)
    def _():
        count_copy().wait_send()
        remote(q_hbm, q_got, s_q, r_q.at[0], d - 4 * s).wait_send()

    @pl.when(hosts)
    def _():
        remote(skew_pack, skew, s_skew, r_skew.at[0], d + 5 * s).wait_send()
        remote(o_send, o_got, s_o, r_o.at[0], d + 4 * s).wait_send()
        remote(lse_send, lse_got, s_lse, r_lse.at[0], d + 4 * s).wait_send()


def shards(n_ctx, queries, keys, values, kv_lists, kv_counts):
    rows, width = queries.shape
    heads = width // HEAD
    nblk = kv_lists.shape[3]
    bs = rows // nblk
    half, quarter = nblk // 2 * bs, nblk // 4 * bs
    far_rows = 2 * (nblk // 4 + nblk // 8) * bs
    far_room = far_rows + (-far_rows) % HEAD
    guest_room = rows + half + quarter
    guest_room += (-guest_room) % HEAD
    piece = PIECE_HEADS if heads % PIECE_HEADS == 0 else 1
    pieces = heads // piece
    kv = jnp.bfloat16
    f32 = jnp.float32
    vmem = pl.BlockSpec(memory_space=pltpu.VMEM)
    hbm = pl.BlockSpec(memory_space=pl.ANY)
    smem = pl.BlockSpec(memory_space=pltpu.SMEM)
    dma = pltpu.SemaphoreType.DMA
    return pl.pallas_call(
        functools.partial(body, n_ctx, nblk, piece),
        out_shape=pltpu.VMEM((rows, width), jnp.bfloat16),
        in_specs=[hbm, hbm, hbm, smem, smem],
        out_specs=vmem,
        scratch_shapes=[
            pltpu.VMEM((rows, width), kv),
            pltpu.VMEM((nblk, bs, width), kv),
            pltpu.VMEM((nblk, bs, width), kv),
            pltpu.VMEM((2, nblk, bs, width), kv),
            pltpu.VMEM((2, nblk, bs, width), kv),
            pltpu.VMEM((2, nblk, bs, width), kv),
            pltpu.VMEM((2, half // bs, bs, width), kv),
            pltpu.VMEM((2, half // bs, bs, width), kv),
            pltpu.VMEM((2, far_room // bs, bs, width), kv),
            pltpu.VMEM((2, far_rows // bs, bs, width), kv),
            pltpu.VMEM((2, nblk, bs, piece * HEAD), kv),
            pltpu.VMEM((rows, width), kv),
            pltpu.VMEM((rows, width), kv),
            pltpu.VMEM((rows, width), kv),
            pltpu.VMEM((heads, 8, rows), f32),
            pltpu.VMEM((heads, 8, rows), f32),
            pltpu.VMEM((heads, rows, HEAD), f32),
            pltpu.VMEM((heads, rows, HEAD), f32),
            pltpu.VMEM((heads, rows, HEAD), f32),
            pltpu.VMEM((1, rows), f32),
            pltpu.VMEM((1, far_room + 2 * half + rows), f32),
            pltpu.VMEM((1, guest_room), f32),
            pltpu.SMEM((5,) + kv_lists.shape[1:], jnp.int32),
            pltpu.SMEM((1, kv_counts.shape[2], kv_counts.shape[1]), jnp.int32),
            pltpu.SemaphoreType.REGULAR((2,)),
            dma((5,)), dma, dma((2,)), dma, dma, dma, dma((4,)), dma, dma, dma,
            dma((3,)), dma((5,)), dma, dma((2,)), dma((2, pieces)), dma((pieces,)), dma((pieces,)),
            dma((4, pieces)), dma((pieces,)), dma((pieces,)), dma((pieces,)),
        ],
        compiler_params=pltpu.CompilerParams(
            collective_id=0, has_side_effects=True, vmem_limit_bytes=60 * 1024 * 1024
        ),
        name="radial",
    )(
        queries, keys.reshape(nblk, bs, width), values.reshape(nblk, bs, width),
        kv_lists, jnp.swapaxes(kv_counts, 1, 2),
    )


def solution(mesh):
    in_specs = (
        P(("groups", "ctx"), None),
        P(("groups", "ctx"), None),
        P(("groups", "ctx"), None),
        P("ctx", None, None, None),
        P("ctx", None, None),
    )
    out_specs = P(("groups", "ctx"), None)
    return jax.shard_map(
        functools.partial(shards, mesh.shape["ctx"]),
        mesh=mesh, in_specs=in_specs, out_specs=out_specs, check_vma=False,
    )
```

```python
import functools
import math

import jax
import jax.numpy as jnp
from jax import lax
from jax.experimental import pallas as pl
from jax.experimental.pallas import tpu as pltpu
from jax.sharding import PartitionSpec as P

HEAD = 128
MASKED = -1e30
PIECE_HEADS = 2
DETOUR = 1
FORWARD_AT = 1
MESH = pl.DeviceIdType.MESH


def body(
    n_ctx, nblk, piece,
    q_hbm, k_hbm, v_hbm, lists, counts, out_ref,
    q_ref, k_ref, v_ref,
    near, across, passed, relay, edge_pack, skew, skew_pack, far, far_pack, stage,
    q_got, o_send, o_got, lse_send, lse_got,
    acc, top, tot, bias_near, bias_late, bias_guest, lists_got, counts_got, ready,
    s_list, s_count, s_near, s_across, s_relay, s_passed, s_skew, s_far, s_q, s_o, s_lse,
    r_own, r_list, r_count, r_near, r_across, r_relay, r_passed, r_skew, r_far, r_q, r_o, r_lse,
):
    own = [
        pltpu.make_async_copy(src, dst, r_own.at[i])
        for i, (src, dst) in enumerate(((k_hbm, k_ref), (v_hbm, v_ref), (q_hbm, q_ref)))
    ]
    for copy in own:
        copy.start()
    rows, width = q_ref.shape
    heads = width // HEAD
    bs = rows // nblk
    cap1, cap2, cap3 = nblk // 2, nblk // 4, nblk // 8
    rate = math.log2(math.e) / math.sqrt(HEAD)
    cols_piece = piece * HEAD
    pieces = heads // piece
    far_room = far.shape[1] * bs

    d = lax.axis_index("ctx")
    place = lax.rem(d, 4)
    quad = d // 4
    quads = n_ctx // 4
    left = place < 2
    s = jnp.where(left, 1, -1)
    gate = (place == 1) | (place == 2)
    outer = jnp.logical_not(gate)
    has_out = jnp.where(left, quad > 0, quad < quads - 1)
    has_in = jnp.where(left, quad < quads - 1, quad > 0)
    side_in = jnp.where(left, 1, 0)
    side_out = 1 - side_in
    twin = jnp.where(gate, d - s, d + s)
    across_to = jnp.where(gate, d + s, d + 3 * s)
    hosts = outer & has_in
    guests = outer & has_out
    gets_skew = gate & has_out
    edge = outer & jnp.logical_not(has_out)
    gets_edge = outer & jnp.logical_not(has_in)
    asks_edge = gate & jnp.logical_not(has_in)
    detours = gate & has_out
    most = relay.shape[3] // cols_piece
    n_detour = jnp.where(
        detours, jnp.minimum(DETOUR * jnp.where(left, quads - quad, quad + 1), most), 0
    )
    n_relay = jnp.where(
        detours, jnp.minimum(DETOUR * jnp.where(left, quad, quads - 1 - quad), most), 0
    )

    fars = []
    for distance in (4, 8):
        fars.append((d + distance, d + distance < n_ctx))
        fars.append((d - distance, d - distance >= 0))
    arrives = [fars[1], fars[0], fars[3], fars[2]]
    far_rows = (cap2 * bs, cap2 * bs, cap3 * bs, cap3 * bs)
    far_start = (0, cap2 * bs, 2 * cap2 * bs, (2 * cap2 + cap3) * bs)
    far_blocks = [pl.ds(a // bs, n // bs) for a, n in zip(far_start, far_rows)]
    hosted = (outer & left, outer & jnp.logical_not(left), jnp.bool_(False), jnp.bool_(False))
    far_sends = [ok & jnp.logical_not(hosted[i]) for i, (_, ok) in enumerate(fars)]
    far_gets = [ok & jnp.logical_not(hosted[i]) for i, (_, ok) in enumerate(arrives)]
    guest_slot = jnp.where(left, 0, 1)

    def to(device):
        return {"ctx": device}

    barrier = pltpu.get_barrier_semaphore()
    always = jnp.bool_(True)
    partners = [(p, ok) for p, ok in fars[:2]]
    partners += [
        (twin, always),
        (across_to, always),
        (d + 5 * s, hosts),
        (d - 5 * s, gets_skew),
        (d - 3 * s, detours),
        (d + 2 * s, edge | asks_edge),
    ]
    count = jnp.int32(0)
    for p, ok in partners:
        count = count + ok.astype(jnp.int32)

        @pl.when(ok)
        def _(p=p):
            pl.semaphore_signal(barrier, inc=1, device_id=to(p), device_id_type=MESH)

    pl.semaphore_wait(barrier, count)

    @pl.when(fars[0][1] & fars[1][1])
    def _():
        for i in range(2):
            pl.semaphore_signal(
                ready.at[1 - i], inc=1, device_id=to(fars[i][0]), device_id_type=MESH
            )

    def remote(src, dst, ssem, rsem, device):
        return pltpu.make_async_remote_copy(
            src_ref=src, dst_ref=dst, send_sem=ssem, recv_sem=rsem,
            device_id=to(device), device_id_type=MESH,
        )

    def span(c):
        return pl.ds(pl.multiple_of(c * cols_piece, cols_piece), cols_piece)

    flip = (1, 0, 3, 2)

    def list_copy(slot, device):
        return remote(lists.at[0], lists_got.at[slot], s_list.at[slot], r_list.at[slot], device)

    def count_copy():
        return remote(counts, counts_got, s_count, r_count, d - 4 * s)

    def near_copy(kv):
        return remote((k_hbm, v_hbm)[kv], near.at[kv], s_near.at[kv], r_near.at[kv], twin)

    def across_copy(c, kv):
        x = span(c)
        return remote(
            (k_hbm, v_hbm)[kv].at[:, :, x], across.at[kv, :, :, x], s_across, r_across.at[kv, c], across_to
        )

    def edge_copy(c, kv):
        x = span(c)
        return remote(
            edge_pack.at[kv, :, :, x], across.at[kv, pl.ds(0, cap1), :, x],
            s_across, r_across.at[kv, c], across_to,
        )

    def detour_copy(i, kv):
        return remote(
            (k_hbm, v_hbm)[kv].at[:, :, span(pieces - n_detour + i)],
            relay.at[kv, :, :, span(i)], s_across, r_relay.at[kv, i], d - 3 * s,
        )

    def detour_wait(i, kv):
        x = relay.at[kv, :, :, span(i)]
        remote(x, x, s_across, r_relay.at[kv, i], d - 3 * s).wait_recv()

    def relay_copy(i, kv):
        c = pieces - n_relay + i
        return remote(
            relay.at[kv, :, :, span(i)], across.at[kv, :, :, span(c)],
            s_relay.at[kv, i], r_across.at[kv, c], d - 4 * s,
        )

    def passed_copy(c):
        x = span(c)
        return remote(across.at[:, :, :, x], passed.at[:, :, :, x], s_passed, r_passed.at[c], twin)

    def skew_copy(c):
        x = span(c)
        return remote(skew_pack.at[:, :, :, x], skew.at[:, :, :, x], s_skew, r_skew.at[c], d + 5 * s)

    def far_copy(i, c):
        r, x = far_blocks[i], span(c)
        return remote(
            far_pack.at[:, r, :, x], far.at[:, r, :, x], s_far.at[i], r_far.at[i, c], fars[i][0]
        )

    def q_copy(c):
        x = span(c)
        return remote(q_hbm.at[:, x], q_got.at[:, x], s_q, r_q.at[c], d - 4 * s)

    def o_copy(h):
        x = head_cols(h)
        return remote(o_send.at[:, x], o_got.at[:, x], s_o, r_o.at[h], d + 4 * s)

    def lse_copy(h):
        return remote(lse_send.at[h], lse_got.at[h], s_lse, r_lse.at[h], d + 4 * s)

    def each_piece(one, n=pieces):
        def step(c, carry):
            one(c)
            return carry

        lax.fori_loop(0, n, step, 0)

    list_sends = [(flip[i], p, ok) for i, (p, ok) in enumerate(fars)] + [
        (4, d - 5 * s, gets_skew), (5, d + 2 * s, asks_edge)
    ]
    list_gets = [(i, p, ok) for i, (p, ok) in enumerate(fars)] + [
        (4, d + 5 * s, hosts), (5, d + 2 * s, edge)
    ]
    for slot, p, ok in list_sends:
        if slot not in (2, 3):
            @pl.when(ok)
            def _(slot=slot, p=p):
                list_copy(slot, p).start()

    @pl.when(guests)
    def _():
        count_copy().start()

    def start_detour(i):
        for kv in range(2):
            detour_copy(i, kv).start()

    def start_across(c):
        for kv in range(2):
            across_copy(c, kv).start()

    each_piece(start_detour, n_detour)
    each_piece(start_across, jnp.where(edge, 0, pieces - n_detour))
    for kv in range(2):
        near_copy(kv).start()

    for i in range(2):
        @pl.when(fars[2 + i][1])
        def _(i=i):
            pl.semaphore_wait(ready.at[i], 1)
            list_copy(flip[2 + i], fars[2 + i][0]).start()

    for i in range(4):
        @pl.when(jnp.logical_not(far_gets[i]))
        def _(i=i):
            for kv in range(2):
                far[kv, far_blocks[i]] = jnp.zeros((far_rows[i] // bs, bs, width), far.dtype)

    spare = far_room - sum(far_rows)
    if spare:
        for kv in range(2):
            far[kv, pl.ds(sum(far_rows) // bs, spare // bs)] = jnp.zeros(
                (spare // bs, bs, width), far.dtype
            )

    @pl.when(gate & jnp.logical_not(has_out))
    def _():
        for kv in range(2):
            skew[kv] = jnp.zeros(skew.shape[1:], skew.dtype)

    @pl.when(outer & jnp.logical_not(has_out))
    def _():
        o_got[...] = jnp.zeros(o_got.shape, o_got.dtype)
        lse_got[...] = jnp.full(lse_got.shape, MASKED, lse_got.dtype)

    for copy in own:
        copy.wait()

    def flat(x):
        return x.reshape(x.shape[0] * x.shape[1], x.shape[2])

    for i, p, ok in list_gets:
        @pl.when(ok)
        def _(i=i, p=p):
            list_copy(i, p).wait_recv()
            if i < 4:
                for j in range(far_rows[i] // bs):
                    source = lists_got[i, 2 + i // 2, i % 2, j]
                    far_pack[0, far_start[i] // bs + j] = k_ref[source]
                    far_pack[1, far_start[i] // bs + j] = v_ref[source]

    @pl.when(edge)
    def _():
        for j in range(cap1):
            source = lists_got[5, 1, side_out, j]
            edge_pack[0, j] = k_ref[source]
            edge_pack[1, j] = v_ref[source]

        def start_edge(c):
            for kv in range(2):
                edge_copy(c, kv).start()

        each_piece(start_edge)

    @pl.when(hosts)
    def _():
        count_copy().wait_recv()

    def start_far(c):
        @pl.when(guests)
        def _():
            q_copy(c).start()

        for i in range(4):
            @pl.when(far_sends[i])
            def _(i=i):
                far_copy(i, c).start()

    each_piece(start_far)

    def as_bias(seen):
        return jnp.where(seen, 0.0, MASKED).astype(jnp.float32)

    def full_bias(listed, counted):
        block = lax.broadcasted_iota(jnp.int32, (1, rows), 1) // bs
        seen = jnp.zeros((1, rows), jnp.int32)
        for j in range(nblk):
            hit = (block == listed(j)) & (jnp.full((1, rows), j) < counted)
            seen = seen + hit.astype(jnp.int32)
        return as_bias(seen > 0)

    def listed_bias(n, counted):
        column = lax.broadcasted_iota(jnp.int32, (1, n), 1)
        return as_bias(column < counted * bs)

    half = cap1 * bs
    quarter = cap2 * bs
    side_near = jnp.where(gate, side_out, side_in)
    bias_near[...] = full_bias(lambda j: lists[0, 0, side_near, j], counts[0, side_near, 0])
    column = lax.broadcasted_iota(jnp.int32, (1, far_room), 1)
    limit = jnp.zeros(column.shape, jnp.int32)
    for i in range(4):
        shown = jnp.where(far_gets[i], counts[0, i % 2, 2 + i // 2], 0)
        limit = jnp.where(column >= far_start[i], far_start[i] + shown * bs, limit)
    limit = jnp.where(column >= sum(far_rows), 0, limit)
    bias_late[:, :far_room] = as_bias(column < limit)
    bias_late[:, far_room:far_room + half] = listed_bias(half, counts[0, side_in, 1])
    bias_late[:, far_room + half:far_room + 2 * half] = listed_bias(half, counts[0, side_out, 1])
    bias_late[:, far_room + 2 * half:] = full_bias(
        lambda j: lists[0, 0, side_in, j], counts[0, side_in, 0]
    )

    @pl.when(hosts)
    def _():
        bias_guest[:, :rows] = full_bias(
            lambda j: lists_got[guest_slot, 0, side_out, j], counts_got[0, side_out, 0]
        )
        bias_guest[:, rows:rows + half] = listed_bias(half, counts_got[0, side_out, 1])
        bias_guest[:, rows + half:] = listed_bias(
            bias_guest.shape[1] - rows - half, counts_got[0, side_out, 2]
        )

    def wide(x, n):
        return jnp.concatenate([x] * (n // HEAD), axis=1)

    def folded(p):
        total = p[:, :HEAD]
        for i in range(1, p.shape[1] // HEAD):
            total = total + p[:, i * HEAD:(i + 1) * HEAD]
        return total

    def scores(q, k):
        return lax.dot_general(
            q, k, (((1,), (1,)), ((), ())), preferred_element_type=jnp.float32
        ) * rate

    def weigh(sc, v, old=None):
        n = sc.shape[1]
        best = jnp.broadcast_to(jnp.max(sc, axis=1, keepdims=True), (rows, HEAD))
        if old is not None:
            best = jnp.maximum(old, best)
        p = jnp.exp2(sc - wide(best, n))
        mixed = jnp.dot(p.astype(jnp.bfloat16), v, preferred_element_type=jnp.float32)
        return best, folded(p), mixed

    def head_cols(h):
        return pl.ds(pl.multiple_of(h * HEAD, HEAD), HEAD)

    together = max(n for n in (1, 2, 3, 4, 5) if heads % n == 0)

    for kv in range(2):
        near_copy(kv).wait_recv()

    def early(h):
        x = head_cols(h)
        q = q_ref[:, x]
        sc = jnp.concatenate(
            [scores(q, flat(k_ref[:, :, x])), scores(q, flat(near[0, :, :, x])) + bias_near[...]], axis=1
        )
        top[h], tot[h], acc[h] = weigh(
            sc, jnp.concatenate([flat(v_ref[:, :, x]), flat(near[1, :, :, x])], axis=0)
        )

    def early_step(i, carry):
        for u in range(together):
            early(together * i + u)
        return carry

    lax.fori_loop(0, heads // together, early_step, 0)

    def listed(kv, level, side, n, x, of):
        return jnp.concatenate(
            [stage[kv, of(level, side, j), :, x] for j in range(n)], axis=0
        )

    def mine(level, side, j):
        return jnp.where(asks_edge, j, lists[0, level, side, j])

    def theirs(level, side, j):
        return lists_got[guest_slot, level, side, j]

    def wait_far(c):
        for i in range(4):
            @pl.when(far_gets[i])
            def _(i=i):
                far_copy(i, c).wait_recv()

    def late(h, u, n_bias, extra):
        x = head_cols(h)
        y = pl.ds(u * HEAD, HEAD)
        k = [flat(far[0, :, :, x]), listed(0, 1, side_in, cap1, y, mine)]
        v = [flat(far[1, :, :, x]), listed(1, 1, side_in, cap1, y, mine)]
        if extra:
            k += [flat(skew[0, :, :, x]), flat(across[0, :, :, x])]
            v += [flat(skew[1, :, :, x]), flat(across[1, :, :, x])]
        sc = scores(q_ref[:, x], jnp.concatenate(k, axis=0)) + bias_late[:, :n_bias]
        old = top[h]
        best, total, mixed = weigh(sc, jnp.concatenate(v, axis=0), old)
        factor = jnp.exp2(old - best)
        return best, tot[h] * factor + total, acc[h] * factor + mixed

    def gate_piece(c):
        passed_copy(c).wait_recv()
        wait_far(c)

        @pl.when(has_out)
        def _():
            skew_copy(c).wait_recv()

        stage[...] = passed[:, :, :, span(c)]
        for u in range(piece):
            h = c * piece + u
            _, total, mixed = late(h, u, bias_late.shape[1], True)
            total = jnp.sum(total, axis=1, keepdims=True)
            out_ref[:, head_cols(h)] = (mixed / total).astype(out_ref.dtype)

    def send_skew(c):
        x = span(c)
        stage[...] = across[:, :, :, x]
        for kv in range(2):
            for j in range(cap1):
                skew_pack[kv, j, :, x] = stage[kv, lists_got[4, 1, side_out, j]]
        skew_copy(c).start()

    pad = bias_guest.shape[1] - rows - half - quarter

    def host(c):
        q_copy(c).wait_recv()
        for u in range(piece):
            h = c * piece + u
            x = head_cols(h)
            y = pl.ds(u * HEAD, HEAD)
            sides = []
            for kv, mine_ref in enumerate((k_ref, v_ref)):
                parts = [flat(across[kv, :, :, x]), listed(kv, 1, side_out, cap1, y, theirs)]
                parts += [mine_ref[theirs(2, side_out, j), :, x] for j in range(cap2)]
                if pad:
                    parts.append(jnp.zeros((pad, HEAD), across.dtype))
                sides.append(jnp.concatenate(parts, axis=0))
            sc = scores(q_got[:, x], sides[0]) + bias_guest[...]
            best, total, mixed = weigh(sc, sides[1])
            total = jnp.broadcast_to(jnp.sum(total, axis=1, keepdims=True), (rows, HEAD))
            o_send[:, x] = (mixed / total).astype(o_send.dtype)
            lse = best + jnp.log2(total)
            lse_send[h] = jnp.transpose(lse)[:8, :]
            o_copy(h).start()
            lse_copy(h).start()

    def outer_piece(c):
        @pl.when(has_in)
        def _():
            send_skew(c)

        passed_copy(c).wait_recv()
        stage[...] = passed[:, :, :, span(c)]

        @pl.when(has_in)
        def _():
            host(c)

        wait_far(c)
        for u in range(piece):
            h = c * piece + u
            top[h], tot[h], acc[h] = late(h, u, far_room + half, False)

    def outer_finish(c):
        for u in range(piece):
            h = c * piece + u

            @pl.when(has_out)
            def _(h=h):
                o_copy(h).wait_recv()
                lse_copy(h).wait_recv()

            x = head_cols(h)
            lse = jnp.transpose(jnp.broadcast_to(lse_got[h][:1, :], (HEAD, rows)))
            old = top[h]
            best = jnp.maximum(old, lse)
            factor, guest = jnp.exp2(old - best), jnp.exp2(lse - best)
            total = jnp.sum(tot[h], axis=1, keepdims=True) * factor + guest
            mixed = acc[h] * factor + o_got[:, x].astype(jnp.float32) * guest
            out_ref[:, x] = (mixed / total).astype(out_ref.dtype)

    def turn(c, carry):
        @pl.when(c < pieces)
        def _():
            for kv in range(2):
                @pl.when(gets_edge)
                def _(kv=kv):
                    edge_copy(c, kv).wait_recv()

                @pl.when(jnp.logical_not(gets_edge))
                def _(kv=kv):
                    across_copy(c, kv).wait_recv()

            passed_copy(c).start()

            @pl.when((c >= FORWARD_AT) & (c < FORWARD_AT + n_relay))
            def _():
                for kv in range(2):
                    detour_wait(c - FORWARD_AT, kv)
                    relay_copy(c - FORWARD_AT, kv).start()

            @pl.when(outer)
            def _():
                outer_piece(c)

        @pl.when(c > 0)
        def _():
            @pl.when(gate)
            def _():
                gate_piece(c - 1)

            @pl.when(outer)
            def _():
                outer_finish(c - 1)

        return carry

    lax.fori_loop(0, pieces + 1, turn, 0)

    for slot, p, ok in list_sends:
        @pl.when(ok)
        def _(slot=slot, p=p):
            list_copy(slot, p).wait_send()

    for kv in range(2):
        near_copy(kv).wait_send()
    @pl.when(edge)
    def _():
        remote(
            edge_pack, across.at[:, pl.ds(0, cap1)], s_across, r_across.at[0, 0], across_to
        ).wait_send()

    @pl.when(jnp.logical_not(edge))
    def _():
        remote(across, across, s_across, r_across.at[0, 0], across_to).wait_send()

    def end_relay(i):
        for kv in range(2):
            relay_copy(i, kv).wait_send()

    each_piece(end_relay, n_relay)
    remote(across, passed, s_passed, r_passed.at[0], twin).wait_send()
    for i in range(4):
        @pl.when(far_sends[i])
        def _(i=i):
            r = far_blocks[i]
            remote(
                far_pack.at[:, r], far.at[:, r], s_far.at[i], r_far.at[i, 0], fars[i][0]
            ).wait_send()

    @pl.when(guests)
    def _():
        count_copy().wait_send()
        remote(q_hbm, q_got, s_q, r_q.at[0], d - 4 * s).wait_send()

    @pl.when(hosts)
    def _():
        remote(skew_pack, skew, s_skew, r_skew.at[0], d + 5 * s).wait_send()
        remote(o_send, o_got, s_o, r_o.at[0], d + 4 * s).wait_send()
        remote(lse_send, lse_got, s_lse, r_lse.at[0], d + 4 * s).wait_send()


def shards(n_ctx, queries, keys, values, kv_lists, kv_counts):
    rows, width = queries.shape
    heads = width // HEAD
    nblk = kv_lists.shape[3]
    bs = rows // nblk
    half, quarter = nblk // 2 * bs, nblk // 4 * bs
    far_rows = 2 * (nblk // 4 + nblk // 8) * bs
    far_room = far_rows + (-far_rows) % HEAD
    guest_room = rows + half + quarter
    guest_room += (-guest_room) % HEAD
    piece = PIECE_HEADS if heads % PIECE_HEADS == 0 else 1
    pieces = heads // piece
    most = max(1, min(DETOUR * (n_ctx // 4 - 1), pieces // 3))
    kv = jnp.bfloat16
    f32 = jnp.float32
    vmem = pl.BlockSpec(memory_space=pltpu.VMEM)
    hbm = pl.BlockSpec(memory_space=pl.ANY)
    smem = pl.BlockSpec(memory_space=pltpu.SMEM)
    dma = pltpu.SemaphoreType.DMA
    return pl.pallas_call(
        functools.partial(body, n_ctx, nblk, piece),
        out_shape=pltpu.VMEM((rows, width), jnp.bfloat16),
        in_specs=[hbm, hbm, hbm, smem, smem],
        out_specs=vmem,
        scratch_shapes=[
            pltpu.VMEM((rows, width), kv),
            pltpu.VMEM((nblk, bs, width), kv),
            pltpu.VMEM((nblk, bs, width), kv),
            pltpu.VMEM((2, nblk, bs, width), kv),
            pltpu.VMEM((2, nblk, bs, width), kv),
            pltpu.VMEM((2, nblk, bs, width), kv),
            pltpu.VMEM((2, nblk, bs, most * piece * HEAD), kv),
            pltpu.VMEM((2, half // bs, bs, width), kv),
            pltpu.VMEM((2, half // bs, bs, width), kv),
            pltpu.VMEM((2, half // bs, bs, width), kv),
            pltpu.VMEM((2, far_room // bs, bs, width), kv),
            pltpu.VMEM((2, far_rows // bs, bs, width), kv),
            pltpu.VMEM((2, nblk, bs, piece * HEAD), kv),
            pltpu.VMEM((rows, width), kv),
            pltpu.VMEM((rows, width), kv),
            pltpu.VMEM((rows, width), kv),
            pltpu.VMEM((heads, 8, rows), f32),
            pltpu.VMEM((heads, 8, rows), f32),
            pltpu.VMEM((heads, rows, HEAD), f32),
            pltpu.VMEM((heads, rows, HEAD), f32),
            pltpu.VMEM((heads, rows, HEAD), f32),
            pltpu.VMEM((1, rows), f32),
            pltpu.VMEM((1, far_room + 2 * half + rows), f32),
            pltpu.VMEM((1, guest_room), f32),
            pltpu.SMEM((6,) + kv_lists.shape[1:], jnp.int32),
            pltpu.SMEM((1, kv_counts.shape[2], kv_counts.shape[1]), jnp.int32),
            pltpu.SemaphoreType.REGULAR((2,)),
            dma((6,)), dma, dma((2,)), dma, dma((2, most)), dma, dma, dma((4,)), dma, dma, dma,
            dma((3,)), dma((6,)), dma, dma((2,)), dma((2, pieces)), dma((2, most)), dma((pieces,)), dma((pieces,)),
            dma((4, pieces)), dma((pieces,)), dma((heads,)), dma((heads,)),
        ],
        compiler_params=pltpu.CompilerParams(
            collective_id=0, has_side_effects=True, vmem_limit_bytes=60 * 1024 * 1024
        ),
        name="radial",
    )(
        queries, keys.reshape(nblk, bs, width), values.reshape(nblk, bs, width),
        kv_lists, jnp.swapaxes(kv_counts, 1, 2),
    )


def solution(mesh):
    in_specs = (
        P(("groups", "ctx"), None),
        P(("groups", "ctx"), None),
        P(("groups", "ctx"), None),
        P("ctx", None, None, None),
        P("ctx", None, None),
    )
    out_specs = P(("groups", "ctx"), None)
    return jax.shard_map(
        functools.partial(shards, mesh.shape["ctx"]),
        mesh=mesh, in_specs=in_specs, out_specs=out_specs, check_vma=False,
    )
```
